256 devices in a mesh: grp: 2 (over core), dev: 128 (over x, y, z).
Axes of the slice: x: 4, y: 4, z: 8, core: 2. Of those that a mesh axis runs over, the one named last changes fastest.
Arguments:
- coarse_emb: bfloat16 [131072, 128], P('dev'), may hold values from -6 to 6
- req_ids: int32 [128, 2, 128, 16], P('dev', 'grp'), may hold values from 0 to 1023, as said below
- fine_slot: int32 [128, 2, 2048], P('dev', 'grp'), may hold values from 0 to 2047, as said below
- tiles: bfloat16 [4096, 2, 8, 128, 128], P('dev', 'grp'), may hold values from -0.125 to 0.125
- tile_cols: int32 [4096, 2, 8], P('dev', 'grp'), may hold values from 0 to 47
Outputs:
- smoothed: bfloat16 [524288, 128], P('dev')
The draws below stay inside these ranges and needn't reach their ends.
Inputs may be any that keep to these rules, and one draw needn't show every extreme that they name: For each d, g and o only the first entries of req_ids[d, g, o] are requested, at most 16 of them, and for each d and g some owner o has all 16; the remaining entries are 0. fine_slot[d, g, i] = o * 16 + j always names a requested entry j of req_ids[d, g, o], and every requested entry is named by some fine node.
All inputs are finite; a program needn't handle non-finite values.
Results may differ from the reference program's by a relative error of at most 0.001.
Values may be sent and summed in bfloat16 or wider, within the bound.
No kernel may reach another device: no remote copies, remote signals or barrier semaphores. Data moves between devices by JAX's collectives and lax.ppermute only.
A program may use at most 64 MiB of HBM per device.

```python
import jax
import jax.numpy as jnp
from jax import lax

W = 128
B = 128
TPR = 8
CAP = 16
FINE_DEV = 4096
COARSE_DEV = 1024
HALF = 2048
NB = 32
F = 524288
NC = 131072
NBT = 4096
N_GRP = 2
N_DEV = 128


def request_plan(key):
    base_key = jax.random.fold_in(key, 4242)
    k_count, k_heavy, k_start, k_stride = jax.random.split(base_key, 4)
    half_rows = FINE_DEV // N_GRP
    most_live = min(CAP, (half_rows - CAP) // max(N_DEV - 1, 1))
    least_live = min(CAP // 2, most_live)
    counts = jax.random.randint(k_count, (N_DEV, N_GRP, N_DEV), least_live, most_live + 1)
    heavy_owner = jax.random.randint(k_heavy, (N_DEV, N_GRP, 1), 0, N_DEV)
    owner_ids = jnp.arange(N_DEV, dtype=jnp.int32)
    counts = jnp.where(owner_ids[None, None, :] == heavy_owner, CAP, counts)
    start_row = jax.random.randint(k_start, (N_DEV, N_GRP, N_DEV, 1), 0, COARSE_DEV)
    stride = 2 * jax.random.randint(k_stride, (N_DEV, N_GRP, N_DEV, 1), 0, COARSE_DEV // 2) + 1
    slot_ids = jnp.arange(CAP, dtype=jnp.int32)
    row_ids = (start_row + slot_ids[None, None, None, :] * stride) % COARSE_DEV
    live_slots = slot_ids[None, None, None, :] < counts[..., None]
    row_ids = jnp.where(live_slots, row_ids, 0)
    return (row_ids.astype(jnp.int32), live_slots)


def draw_req_ids(key, part):
    return request_plan(key)[0]


def draw_fine_slot(key, part):
    row_ids, live_slots = request_plan(key)
    k_fill, k_order = jax.random.split(jax.random.fold_in(key, 77), 2)
    half_rows = FINE_DEV // N_GRP
    row_count = N_DEV * N_GRP
    live_flat = live_slots.reshape(row_count, N_DEV * CAP).astype(jnp.int32)
    slot_order = jnp.argsort(1 - live_flat, axis=1, stable=True).astype(jnp.int32)
    live_count = jnp.sum(live_flat, axis=1)
    positions = jnp.arange(half_rows, dtype=jnp.int32)[None, :]
    extra_pick = jax.random.randint(k_fill, (row_count, half_rows), 0, live_count[:, None])
    slot_index = jnp.where(positions < live_count[:, None], positions, extra_pick)
    chosen = jnp.take_along_axis(slot_order, slot_index, axis=1)
    shuffle_keys = jax.random.randint(k_order, (row_count, half_rows), 0, 2 ** 16) * half_rows + positions
    shuffle = jnp.argsort(shuffle_keys, axis=1, stable=True)
    chosen = jnp.take_along_axis(chosen, shuffle, axis=1)
    return chosen.reshape(N_DEV, N_GRP, half_rows).astype(jnp.int32)


def plant(entries, stream_key, least, top_value):
    spot = [jax.random.randint(jax.random.fold_in(stream_key, axis), (), 0, length) for axis, length in enumerate(entries.shape)]
    widest = entries.shape.index(max(entries.shape))
    next_to = spot[:widest] + [(spot[widest] + 1) % entries.shape[widest]] + spot[widest + 1:]
    return entries.at[tuple(spot)].set(least).at[tuple(next_to)].set(top_value)


def block_scale(key, dims, cuts, smallest, high):
    def one(axis_at, parts):
        draws = jax.random.uniform(jax.random.fold_in(jax.random.fold_in(key, 6), axis_at), (parts,), jnp.float32, smallest / len(cuts), high / len(cuts))
        return jnp.repeat(jnp.exp(draws), dims[axis_at] // parts).reshape((-1,) + (1,) * (len(dims) - axis_at - 1))

    factor_of = one(*cuts[0])
    for cut in cuts[1:]:
        factor_of = factor_of * one(*cut)
    return factor_of


def bell_draw(key, shape, scale, bound, cuts=(), held_as=jnp.bfloat16):
    entries = jax.random.normal(key, shape, jnp.float32) * scale
    if len(cuts) > 0:
        entries = block_scale(key, shape, cuts, -0.22, 0.18) * entries
    return jnp.clip(entries, min=-bound, max=bound).astype(held_as)


def setup_inputs(seed: int = 0) -> dict:
    seeds = jax.random.split(jax.random.key(seed), 6)
    return {
        "coarse_emb": bell_draw(seeds[0], (NC, W), 1.0, 6.0, ((0, 128),)),
        "req_ids": draw_req_ids(jax.random.fold_in(seeds[5], 71), 0),
        "fine_slot": draw_fine_slot(jax.random.fold_in(seeds[5], 71), 0),
        "tiles": bell_draw(seeds[3], (NBT, N_GRP, TPR, B, B), (B * TPR * N_GRP) ** -0.5, 0.125, ((0, 128), (1, 2))),
        "tile_cols": plant(jax.random.randint(seeds[4], (NBT, N_GRP, TPR), 0, 3 * (HALF // B)), jax.random.fold_in(seeds[4], 1), 0, (3 * (HALF // B)) - 1).astype(jnp.int32),
    }


def reference(coarse_emb, req_ids, fine_slot, tiles, tile_cols):
    owners = jnp.arange(N_DEV, dtype=jnp.int32)[None, None, :, None] * COARSE_DEV
    table_ids = (req_ids + owners).reshape(N_DEV, N_GRP, N_DEV * CAP)
    parent = jnp.take_along_axis(table_ids, fine_slot, axis=2)
    lifted = coarse_emb[parent]
    half_blocks = HALF // B
    blocks = lifted.reshape(N_DEV, N_GRP, half_blocks, B, W)
    zero_rows = jnp.zeros((1, N_GRP, half_blocks, B, W), jnp.bfloat16)
    padded = jnp.concatenate([zero_rows, blocks, zero_rows], axis=0)

    def one_dev(device):
        window = lax.dynamic_slice_in_dim(padded, device, 3, 0)
        extended = jnp.transpose(window, (1, 0, 2, 3, 4)).reshape(N_GRP, 3 * half_blocks, B, W)
        dev_tiles = lax.dynamic_slice_in_dim(tiles, device * NB, NB, 0)
        dev_cols = lax.dynamic_slice_in_dim(tile_cols, device * NB, NB, 0)
        summed = jnp.zeros((NB, B, W), jnp.float32)
        for group in range(N_GRP):
            picked = extended[group][dev_cols[:, group]]
            summed = summed + jnp.einsum("rtij,rtjw->riw", dev_tiles[:, group].astype(jnp.float32), picked.astype(jnp.float32))
        return summed

    tile_sums = lax.map(one_dev, jnp.arange(N_DEV, dtype=jnp.int32)).reshape(F, W)
    result = lifted.reshape(F, W).astype(jnp.float32) - 0.5 * tile_sums
    return result.astype(jnp.bfloat16)
```

```python
import functools

import jax
import jax.numpy as jnp
from jax import lax
from jax.experimental import pallas as pl
from jax.experimental.pallas import tpu as pltpu
from jax.sharding import PartitionSpec as P


LANES = 128
VMEM_SPEC = pl.BlockSpec(memory_space=pltpu.VMEM)
SMEM_SPEC = pl.BlockSpec(memory_space=pltpu.SMEM)
PARAMS = pltpu.CompilerParams(vmem_limit_bytes=16 * 1024 * 1024)
CHUNKS = 2


def column_of(index_ref, b):
    return jnp.transpose(jnp.broadcast_to(index_ref[b : b + 1, :], (LANES, LANES)))


def side_by_side(table_ref):
    rows = table_ref.shape[0]
    return jnp.concatenate([table_ref[: rows // 2, :], table_ref[rows // 2 :, :]], axis=1)


def rows_of(wanted, table, depth):
    lane = lax.broadcasted_iota(jnp.int16, (LANES, LANES), 1)
    one = jnp.ones((LANES, LANES), jnp.bfloat16)
    zero = jnp.zeros((LANES, LANES), jnp.bfloat16)
    low = (wanted & (depth - 1)).astype(jnp.int16)
    onehot = jnp.concatenate(
        [jnp.where(low - jnp.int16(c * LANES) == lane, one, zero) for c in range(depth // LANES)],
        axis=1,
    )
    width = table.shape[1] // 2
    found = jnp.dot(onehot, table, preferred_element_type=jnp.float32)
    return jnp.where(wanted >= depth, found[:, width:], found[:, :width])


def gather_body(asked_ref, table_ref, out_ref):
    slots = asked_ref.shape[2]
    each = LANES // slots
    table = table_ref[...]
    row = lax.broadcasted_iota(jnp.int32, (LANES, slots), 0)
    slot = lax.broadcasted_iota(jnp.int32, (LANES, slots), 1)
    chosen = lax.rem(row, slots) == slot
    for b in range(asked_ref.shape[0] // each):
        spread = jnp.concatenate(
            [jnp.broadcast_to(asked_ref[b * each + k], (slots, slots)) for k in range(each)], axis=0
        )
        wanted = jnp.sum(jnp.where(chosen, spread, 0), axis=1, keepdims=True)
        wanted = jnp.broadcast_to(wanted, (LANES, LANES))
        value = rows_of(wanted, table, table_ref.shape[0])
        out_ref[b * LANES : (b + 1) * LANES, :] = value.astype(out_ref.dtype)


def gather(asked, table):
    count = asked.size
    return pl.pallas_call(
        gather_body,
        out_shape=jax.ShapeDtypeStruct((count, table.shape[1] // 2), table.dtype),
        in_specs=[VMEM_SPEC, VMEM_SPEC],
        out_specs=VMEM_SPEC,
        compiler_params=PARAMS,
        name="gather",
    )(asked, table)


def columns_body(index_ref, *refs, first):
    out_ref = refs[-1]
    for b in range(out_ref.shape[0] // LANES):
        out_ref[b * LANES : (b + 1) * LANES, :] = column_of(index_ref, first + b)
    if len(refs) == 3:
        refs[1][...] = side_by_side(refs[0])


def columns(index, first, count, table=None):
    wide = jax.ShapeDtypeStruct((count * LANES, LANES), jnp.int32)
    shapes, arrays = (wide,), (index,)
    if table is not None:
        rows, width = table.shape
        shapes = (jax.ShapeDtypeStruct((rows // 2, 2 * width), table.dtype), wide)
        arrays = (index, table)
    return pl.pallas_call(
        functools.partial(columns_body, first=first),
        out_shape=shapes,
        in_specs=[VMEM_SPEC] * len(arrays),
        out_specs=(VMEM_SPEC,) * len(shapes),
        compiler_params=PARAMS,
        name="columns",
    )(*arrays)


def lift_body(*refs):
    table_ref, out_ref = refs[-2:]
    table = side_by_side(table_ref)
    start = 0
    for wanted_ref in refs[:-2]:
        for b in range(wanted_ref.shape[0] // LANES):
            rows = slice(b * LANES, (b + 1) * LANES)
            value = rows_of(wanted_ref[rows, :], table, table_ref.shape[0] // 2)
            out_ref[start : start + LANES, :] = value.astype(out_ref.dtype)
            start += LANES


def lift(parts, table):
    return pl.pallas_call(
        lift_body,
        out_shape=jax.ShapeDtypeStruct((sum(p.shape[0] for p in parts), table.shape[1]), table.dtype),
        in_specs=[VMEM_SPEC] * (len(parts) + 1),
        out_specs=VMEM_SPEC,
        compiler_params=PARAMS,
        name="lift",
    )(*parts, table)


def load_body(tiles_ref, out_ref, sems, *, pieces):
    each = tiles_ref.shape[0] // pieces
    copies = [
        pltpu.make_async_copy(
            tiles_ref.at[pl.ds(p * each, each)], out_ref.at[pl.ds(p * each, each)], sems.at[p]
        )
        for p in range(pieces)
    ]
    for copy in copies:
        copy.start()
    for copy in copies:
        copy.wait()


def load(tiles):
    return pl.pallas_call(
        functools.partial(load_body, pieces=4),
        out_shape=pltpu.VMEM(tiles.shape, tiles.dtype),
        in_specs=[pl.BlockSpec(memory_space=pltpu.HBM)],
        out_specs=VMEM_SPEC,
        scratch_shapes=[pltpu.SemaphoreType.DMA((4,))],
        compiler_params=pltpu.CompilerParams(vmem_limit_bytes=48 * 1024 * 1024),
        name="load",
    )(tiles)


def smooth_body(cols_ref, tiles_ref, before_ref, own_ref, after_ref, out_ref, blocks, *, base, count, unroll):
    per_row = tiles_ref.shape[1]
    half = own_ref.shape[0]
    group = lax.axis_index("grp").astype(jnp.int32)
    blocks[0:half] = before_ref[...]
    blocks[half : 2 * half] = own_ref[...]
    blocks[2 * half : 3 * half] = after_ref[...]

    def step(s, carry):
        for k in range(unroll):
            i = s * unroll + k
            r = base + i
            left = jnp.concatenate([tiles_ref[r, t] for t in range(per_row)], axis=1)
            right = jnp.concatenate([blocks[cols_ref[t, r]] for t in range(per_row)], axis=0)
            product = jnp.dot(left, right, preferred_element_type=jnp.float32)
            own = own_ref[lax.rem(r, half)].astype(jnp.float32)
            own = jnp.where(r // half == group, own, 0.0)
            out_ref[pl.ds(pl.multiple_of(i * LANES, LANES), LANES), :] = own - 0.5 * product
        return carry

    lax.fori_loop(0, count // unroll, step, 0)


def smooth(cols, tiles, before, own, after, base, count):
    half = own.shape[0]
    return pl.pallas_call(
        functools.partial(smooth_body, base=base, count=count, unroll=8),
        out_shape=jax.ShapeDtypeStruct((count * LANES, LANES), jnp.float32),
        in_specs=[SMEM_SPEC] + [VMEM_SPEC] * 4,
        out_specs=VMEM_SPEC,
        scratch_shapes=[pltpu.VMEM((3 * half, LANES, LANES), own.dtype)],
        compiler_params=PARAMS,
        name="smooth",
    )(cols, tiles, before, own, after)


def combine_body(*refs):
    out_ref = refs[-1]
    start = 0
    for mine_ref, theirs_ref in zip(refs[:-1:2], refs[1:-1:2]):
        rows = mine_ref.shape[0]
        out_ref[start : start + rows, :] = (mine_ref[...] + theirs_ref[...]).astype(out_ref.dtype)
        start += rows


def combine(pairs, dtype):
    parts = [part for pair in pairs for part in pair]
    rows = sum(mine.shape[0] for mine, _ in pairs)
    return pl.pallas_call(
        combine_body,
        out_shape=jax.ShapeDtypeStruct((rows, parts[0].shape[1]), dtype),
        in_specs=[VMEM_SPEC] * len(parts),
        out_specs=VMEM_SPEC,
        compiler_params=PARAMS,
        name="combine",
    )(*parts)


def per_device(coarse_emb, req_ids, fine_slot, tiles, tile_cols):
    devices = lax.axis_size("dev")
    slots = req_ids.shape[3]
    width = coarse_emb.shape[1]
    row_blocks = tiles.shape[0]
    index = fine_slot.reshape(-1, LANES)
    half = index.shape[0] // 2
    tiles = load(tiles[:, 0])
    asked = lax.all_to_all(
        req_ids.reshape(devices, 1, slots), "dev", split_axis=0, concat_axis=0, tiled=True
    )
    table, first = columns(index, 0, half, coarse_emb)
    wanted = gather(asked, table)
    (second,) = columns(index, half, half)
    received = lax.all_to_all(
        wanted.reshape(devices, slots, width), "dev", split_axis=0, concat_axis=0, tiled=True
    )
    lifted = lift((first, second), received.reshape(devices * slots, width))
    up = [(i, i + 1) for i in range(devices - 1)]
    down = [(i + 1, i) for i in range(devices - 1)]
    before = lax.ppermute(lifted, "dev", up).reshape(-1, LANES, width)
    after = lax.ppermute(lifted, "dev", down).reshape(-1, LANES, width)
    own = lifted.reshape(-1, LANES, width)
    cols = tile_cols[:, 0].T
    each = row_blocks // CHUNKS
    outs = []
    for c in range(CHUNKS):
        mine = smooth(cols, tiles, before, own, after, c * each, each)
        theirs = lax.ppermute(mine, "grp", [(0, 1), (1, 0)])
        outs.append((mine, theirs))
    return combine(outs, lifted.dtype)


def solution(mesh):
    return jax.shard_map(
        per_device,
        mesh=mesh,
        in_specs=(
            P("dev", None),
            P("dev", "grp", None, None),
            P("dev", "grp", None),
            P("dev", "grp", None, None, None),
            P("dev", "grp", None),
        ),
        out_specs=P("dev", None),
        check_vma=False,
    )
```

```python
import functools

import jax
import jax.numpy as jnp
from jax import lax
from jax.experimental import pallas as pl
from jax.experimental.pallas import tpu as pltpu
from jax.sharding import PartitionSpec as P


LANES = 128
VMEM_SPEC = pl.BlockSpec(memory_space=pltpu.VMEM)
SMEM_SPEC = pl.BlockSpec(memory_space=pltpu.SMEM)
PARAMS = pltpu.CompilerParams(vmem_limit_bytes=16 * 1024 * 1024)
CHUNKS = (8, 8, 8, 8)
UNROLL = 8


def column_of(index_ref, b):
    return jnp.transpose(jnp.broadcast_to(index_ref[b : b + 1, :], (LANES, LANES)))


def side_by_side(table_ref):
    rows = table_ref.shape[0]
    return jnp.concatenate([table_ref[: rows // 2, :], table_ref[rows // 2 :, :]], axis=1)


def rows_of(wanted, table, depth):
    lane = lax.broadcasted_iota(jnp.int16, (LANES, LANES), 1)
    one = jnp.ones((LANES, LANES), jnp.bfloat16)
    zero = jnp.zeros((LANES, LANES), jnp.bfloat16)
    low = (wanted & (depth - 1)).astype(jnp.int16)
    onehot = jnp.concatenate(
        [jnp.where(low - jnp.int16(c * LANES) == lane, one, zero) for c in range(depth // LANES)],
        axis=1,
    )
    width = table.shape[1] // 2
    found = jnp.dot(onehot, table, preferred_element_type=jnp.float32)
    return jnp.where(wanted >= depth, found[:, width:], found[:, :width])


def gather_body(asked_ref, table_ref, out_ref):
    slots = asked_ref.shape[2]
    each = LANES // slots
    table = table_ref[...]
    row = lax.broadcasted_iota(jnp.int32, (LANES, slots), 0)
    slot = lax.broadcasted_iota(jnp.int32, (LANES, slots), 1)
    chosen = lax.rem(row, slots) == slot
    for b in range(asked_ref.shape[0] // each):
        spread = jnp.concatenate(
            [jnp.broadcast_to(asked_ref[b * each + k], (slots, slots)) for k in range(each)], axis=0
        )
        wanted = jnp.sum(jnp.where(chosen, spread, 0), axis=1, keepdims=True)
        wanted = jnp.broadcast_to(wanted, (LANES, LANES))
        value = rows_of(wanted, table, table_ref.shape[0])
        out_ref[b * LANES : (b + 1) * LANES, :] = value.astype(out_ref.dtype)


def gather(asked, table):
    count = asked.size
    return pl.pallas_call(
        gather_body,
        out_shape=jax.ShapeDtypeStruct((count, table.shape[1] // 2), table.dtype),
        in_specs=[VMEM_SPEC, VMEM_SPEC],
        out_specs=VMEM_SPEC,
        compiler_params=PARAMS,
        name="gather",
    )(asked, table)


def columns_body(index_ref, *refs, first):
    out_ref = refs[-1]
    for b in range(out_ref.shape[0] // LANES):
        out_ref[b * LANES : (b + 1) * LANES, :] = column_of(index_ref, first + b)
    if len(refs) == 3:
        refs[1][...] = side_by_side(refs[0])


def columns(index, first, count, table=None):
    wide = jax.ShapeDtypeStruct((count * LANES, LANES), jnp.int32)
    shapes, arrays = (wide,), (index,)
    if table is not None:
        rows, width = table.shape
        shapes = (jax.ShapeDtypeStruct((rows // 2, 2 * width), table.dtype), wide)
        arrays = (index, table)
    return pl.pallas_call(
        functools.partial(columns_body, first=first),
        out_shape=shapes,
        in_specs=[VMEM_SPEC] * len(arrays),
        out_specs=(VMEM_SPEC,) * len(shapes),
        compiler_params=PARAMS,
        name="columns",
    )(*arrays)


def lift_body(*refs):
    table_ref, out_ref = refs[-2:]
    table = side_by_side(table_ref)
    start = 0
    for wanted_ref in refs[:-2]:
        for b in range(wanted_ref.shape[0] // LANES):
            rows = slice(b * LANES, (b + 1) * LANES)
            value = rows_of(wanted_ref[rows, :], table, table_ref.shape[0] // 2)
            out_ref[start : start + LANES, :] = value.astype(out_ref.dtype)
            start += LANES


def lift(parts, table):
    return pl.pallas_call(
        lift_body,
        out_shape=jax.ShapeDtypeStruct((sum(p.shape[0] for p in parts), table.shape[1]), table.dtype),
        in_specs=[VMEM_SPEC] * (len(parts) + 1),
        out_specs=VMEM_SPEC,
        compiler_params=PARAMS,
        name="lift",
    )(*parts, table)


def load_body(tiles_ref, out_ref, sems, *, pieces):
    each = tiles_ref.shape[0] // pieces
    copies = [
        pltpu.make_async_copy(
            tiles_ref.at[pl.ds(p * each, each)], out_ref.at[pl.ds(p * each, each)], sems.at[p]
        )
        for p in range(pieces)
    ]
    for copy in copies:
        copy.start()
    for copy in copies:
        copy.wait()


def load(tiles):
    return pl.pallas_call(
        functools.partial(load_body, pieces=4),
        out_shape=pltpu.VMEM(tiles.shape, tiles.dtype),
        in_specs=[pl.BlockSpec(memory_space=pltpu.HBM)],
        out_specs=VMEM_SPEC,
        scratch_shapes=[pltpu.SemaphoreType.DMA((4,))],
        compiler_params=pltpu.CompilerParams(vmem_limit_bytes=48 * 1024 * 1024),
        name="load",
    )(tiles)


def product_rows(cols_ref, tiles_ref, blocks_ref, out_ref, base):
    per_row = tiles_ref.shape[1]
    half = blocks_ref.shape[0] // 3
    count = out_ref.shape[0] // LANES
    group = lax.axis_index("grp").astype(jnp.int32)

    def step(s, carry):
        for k in range(UNROLL):
            i = s * UNROLL + k
            r = base + i
            left = jnp.concatenate([tiles_ref[r, t] for t in range(per_row)], axis=1)
            right = jnp.concatenate([blocks_ref[cols_ref[t, r]] for t in range(per_row)], axis=0)
            product = jnp.dot(left, right, preferred_element_type=jnp.float32)
            own = blocks_ref[half + lax.rem(r, half)].astype(jnp.float32)
            own = jnp.where(r // half == group, own, 0.0)
            out_ref[pl.ds(pl.multiple_of(i * LANES, LANES), LANES), :] = own - 0.5 * product
        return carry

    lax.fori_loop(0, count // UNROLL, step, 0)


def first_body(cols_ref, tiles_ref, before_ref, own_ref, after_ref, out_ref, blocks_ref):
    half = own_ref.shape[0]
    place = lax.axis_index("dev")
    zeros = jnp.zeros(own_ref.shape, own_ref.dtype)
    blocks_ref[0:half] = jnp.where(place > 0, before_ref[...], zeros)
    blocks_ref[half : 2 * half] = own_ref[...]
    blocks_ref[2 * half : 3 * half] = jnp.where(
        place < lax.axis_size("dev") - 1, after_ref[...], zeros
    )
    product_rows(cols_ref, tiles_ref, blocks_ref, out_ref, 0)


def first_rows(cols, tiles, before, own, after, count):
    half = own.shape[0]
    return pl.pallas_call(
        first_body,
        out_shape=(
            jax.ShapeDtypeStruct((count * LANES, LANES), jnp.float32),
            jax.ShapeDtypeStruct((3 * half, LANES, LANES), own.dtype),
        ),
        in_specs=[SMEM_SPEC] + [VMEM_SPEC] * 4,
        out_specs=(VMEM_SPEC, VMEM_SPEC),
        compiler_params=PARAMS,
        name="first_rows",
    )(cols, tiles, before, own, after)


def more_body(cols_ref, tiles_ref, blocks_ref, out_ref, *, base):
    product_rows(cols_ref, tiles_ref, blocks_ref, out_ref, base)


def more_rows(cols, tiles, blocks, base, count):
    return pl.pallas_call(
        functools.partial(more_body, base=base),
        out_shape=jax.ShapeDtypeStruct((count * LANES, LANES), jnp.float32),
        in_specs=[SMEM_SPEC] + [VMEM_SPEC] * 2,
        out_specs=VMEM_SPEC,
        compiler_params=PARAMS,
        name="more_rows",
    )(cols, tiles, blocks)


def combine_body(*refs, first):
    out_ref, buffer, sem = refs[-3:]
    pairs = (len(refs) - 3) // 2
    start = 0
    for mine_ref, theirs_ref in zip(refs[: 2 * pairs : 2], refs[1 : 2 * pairs : 2]):
        rows = mine_ref.shape[0]
        buffer[start : start + rows, :] = (mine_ref[...] + theirs_ref[...]).astype(buffer.dtype)
        start += rows
    copy = pltpu.make_async_copy(buffer, out_ref.at[pl.ds(first, start)], sem)
    copy.start()
    copy.wait()


def combine(pairs, out, rows, first, dtype):
    parts = [part for pair in pairs for part in pair]
    count, width = sum(mine.shape[0] for mine, _ in pairs), parts[0].shape[1]
    anywhere = pl.BlockSpec(memory_space=pltpu.HBM)
    before = [] if out is None else [out]
    return pl.pallas_call(
        functools.partial(combine_body, first=first),
        out_shape=jax.ShapeDtypeStruct((rows, width), dtype),
        in_specs=[VMEM_SPEC] * len(parts) + [anywhere] * len(before),
        out_specs=anywhere,
        input_output_aliases={len(parts): 0} if before else {},
        scratch_shapes=[pltpu.VMEM((count, width), dtype), pltpu.SemaphoreType.DMA],
        compiler_params=PARAMS,
        name="combine",
    )(*parts, *before)


def per_device(coarse_emb, req_ids, fine_slot, tiles, tile_cols):
    devices = lax.axis_size("dev")
    slots = req_ids.shape[3]
    width = coarse_emb.shape[1]
    row_blocks = tiles.shape[0]
    index = fine_slot.reshape(-1, LANES)
    half = index.shape[0] // 2
    tiles = load(tiles[:, 0])
    asked = lax.all_to_all(
        req_ids.reshape(devices, 1, slots), "dev", split_axis=0, concat_axis=0, tiled=True
    )
    table, first = columns(index, 0, half, coarse_emb)
    wanted = gather(asked, table)
    (second,) = columns(index, half, half)
    received = lax.all_to_all(
        wanted.reshape(devices, slots, width), "dev", split_axis=0, concat_axis=0, tiled=True
    )
    lifted = lift((first, second), received.reshape(devices * slots, width))
    up = [(i, i + 1) for i in range(devices - 1)]
    down = [((i + 1) % devices, i) for i in range(devices)]
    before = lax.ppermute(lifted, "dev", up).reshape(-1, LANES, width)
    after = lax.ppermute(lifted, "dev", down).reshape(-1, LANES, width)
    own = lifted.reshape(-1, LANES, width)
    cols = tile_cols[:, 0].T
    parts = []
    base = 0
    for c, count in enumerate(CHUNKS):
        if c == 0:
            mine, blocks = first_rows(cols, tiles, before, own, after, count)
        else:
            mine = more_rows(cols, tiles, blocks, base, count)
        parts.append((mine, lax.ppermute(mine, "grp", [(0, 1), (1, 0)])))
        base += count
    rows = row_blocks * LANES
    out = combine(parts[:-1], None, rows, 0, lifted.dtype)
    return combine(parts[-1:], out, rows, rows - parts[-1][0].shape[0], lifted.dtype)


def solution(mesh):
    return jax.shard_map(
        per_device,
        mesh=mesh,
        in_specs=(
            P("dev", None),
            P("dev", "grp", None, None),
            P("dev", "grp", None),
            P("dev", "grp", None, None, None),
            P("dev", "grp", None),
        ),
        out_specs=P("dev", None),
        check_vma=False,
    )
```

```python
import functools

import jax
import jax.numpy as jnp
from jax import lax
from jax.experimental import pallas as pl
from jax.experimental.pallas import tpu as pltpu
from jax.sharding import PartitionSpec as P


LANES = 128
VMEM_SPEC = pl.BlockSpec(memory_space=pltpu.VMEM)
SMEM_SPEC = pl.BlockSpec(memory_space=pltpu.SMEM)
PARAMS = pltpu.CompilerParams(vmem_limit_bytes=16 * 1024 * 1024)
CHUNKS = (8, 12, 12)


def column_of(index_ref, b):
    return jnp.transpose(jnp.broadcast_to(index_ref[b : b + 1, :], (LANES, LANES)))


def side_by_side(table_ref):
    rows = table_ref.shape[0]
    return jnp.concatenate([table_ref[: rows // 2, :], table_ref[rows // 2 :, :]], axis=1)


def rows_of(wanted, table, depth):
    lane = lax.broadcasted_iota(jnp.int16, (LANES, LANES), 1)
    one = jnp.ones((LANES, LANES), jnp.bfloat16)
    zero = jnp.zeros((LANES, LANES), jnp.bfloat16)
    low = (wanted & (depth - 1)).astype(jnp.int16)
    onehot = jnp.concatenate(
        [jnp.where(low - jnp.int16(c * LANES) == lane, one, zero) for c in range(depth // LANES)],
        axis=1,
    )
    width = table.shape[1] // 2
    found = jnp.dot(onehot, table, preferred_element_type=jnp.float32)
    return jnp.where(wanted >= depth, found[:, width:], found[:, :width])


def gather_body(asked_ref, table_ref, out_ref):
    slots = asked_ref.shape[2]
    each = LANES // slots
    table = table_ref[...]
    row = lax.broadcasted_iota(jnp.int32, (LANES, slots), 0)
    slot = lax.broadcasted_iota(jnp.int32, (LANES, slots), 1)
    chosen = lax.rem(row, slots) == slot
    for b in range(asked_ref.shape[0] // each):
        spread = jnp.concatenate(
            [jnp.broadcast_to(asked_ref[b * each + k], (slots, slots)) for k in range(each)], axis=0
        )
        wanted = jnp.sum(jnp.where(chosen, spread, 0), axis=1, keepdims=True)
        wanted = jnp.broadcast_to(wanted, (LANES, LANES))
        value = rows_of(wanted, table, table_ref.shape[0])
        out_ref[b * LANES : (b + 1) * LANES, :] = value.astype(out_ref.dtype)


def gather(asked, table):
    count = asked.size
    return pl.pallas_call(
        gather_body,
        out_shape=jax.ShapeDtypeStruct((count, table.shape[1] // 2), table.dtype),
        in_specs=[VMEM_SPEC, VMEM_SPEC],
        out_specs=VMEM_SPEC,
        compiler_params=PARAMS,
        name="gather",
    )(asked, table)


def columns_body(index_ref, *refs, first):
    out_ref = refs[-1]
    for b in range(out_ref.shape[0] // LANES):
        out_ref[b * LANES : (b + 1) * LANES, :] = column_of(index_ref, first + b)
    if len(refs) == 3:
        refs[1][...] = side_by_side(refs[0])


def columns(index, first, count, table=None):
    wide = jax.ShapeDtypeStruct((count * LANES, LANES), jnp.int32)
    shapes, arrays = (wide,), (index,)
    if table is not None:
        rows, width = table.shape
        shapes = (jax.ShapeDtypeStruct((rows // 2, 2 * width), table.dtype), wide)
        arrays = (index, table)
    return pl.pallas_call(
        functools.partial(columns_body, first=first),
        out_shape=shapes,
        in_specs=[VMEM_SPEC] * len(arrays),
        out_specs=(VMEM_SPEC,) * len(shapes),
        compiler_params=PARAMS,
        name="columns",
    )(*arrays)


def lift_body(*refs):
    table_ref, out_ref = refs[-2:]
    table = side_by_side(table_ref)
    start = 0
    for wanted_ref in refs[:-2]:
        for b in range(wanted_ref.shape[0] // LANES):
            rows = slice(b * LANES, (b + 1) * LANES)
            value = rows_of(wanted_ref[rows, :], table, table_ref.shape[0] // 2)
            out_ref[start : start + LANES, :] = value.astype(out_ref.dtype)
            start += LANES


def lift(parts, table):
    return pl.pallas_call(
        lift_body,
        out_shape=jax.ShapeDtypeStruct((sum(p.shape[0] for p in parts), table.shape[1]), table.dtype),
        in_specs=[VMEM_SPEC] * (len(parts) + 1),
        out_specs=VMEM_SPEC,
        compiler_params=PARAMS,
        name="lift",
    )(*parts, table)


def load_body(tiles_ref, out_ref, sems, *, pieces):
    each = tiles_ref.shape[0] // pieces
    copies = [
        pltpu.make_async_copy(
            tiles_ref.at[pl.ds(p * each, each)], out_ref.at[pl.ds(p * each, each)], sems.at[p]
        )
        for p in range(pieces)
    ]
    for copy in copies:
        copy.start()
    for copy in copies:
        copy.wait()


def load(tiles):
    return pl.pallas_call(
        functools.partial(load_body, pieces=4),
        out_shape=pltpu.VMEM(tiles.shape, tiles.dtype),
        in_specs=[pl.BlockSpec(memory_space=pltpu.HBM)],
        out_specs=VMEM_SPEC,
        scratch_shapes=[pltpu.SemaphoreType.DMA((4,))],
        compiler_params=pltpu.CompilerParams(vmem_limit_bytes=48 * 1024 * 1024),
        name="load",
    )(tiles)


def product_rows(cols_ref, tiles_ref, blocks_ref, out_ref, base):
    per_row = tiles_ref.shape[1]
    half = blocks_ref.shape[0] // 3
    count = out_ref.shape[0] // LANES
    group = lax.axis_index("grp").astype(jnp.int32)

    for i in range(count):
        r = base + i
        left = jnp.concatenate([tiles_ref[r, t] for t in range(per_row)], axis=1)
        right = jnp.concatenate([blocks_ref[cols_ref[t, r]] for t in range(per_row)], axis=0)
        product = jnp.dot(left, right, preferred_element_type=jnp.float32)
        own = blocks_ref[half + r % half].astype(jnp.float32)
        own = jnp.where(group == r // half, own, 0.0)
        out_ref[i * LANES : (i + 1) * LANES, :] = own - 0.5 * product


def first_body(cols_ref, tiles_ref, outer_ref, own_ref, inner_ref, out_ref, blocks_ref):
    half = own_ref.shape[0]
    place = lax.axis_index("dev")
    odd = lax.rem(place, 2) == 1
    ends = (place == 0) | (place == lax.axis_size("dev") - 1)
    outer = jnp.where(ends, jnp.zeros(own_ref.shape, own_ref.dtype), outer_ref[...])
    blocks_ref[half : 2 * half] = own_ref[...]
    blocks_ref[pl.ds(jnp.where(odd, 2 * half, 0), half)] = outer
    blocks_ref[pl.ds(jnp.where(odd, 0, 2 * half), half)] = inner_ref[...]
    product_rows(cols_ref, tiles_ref, blocks_ref, out_ref, 0)


def first_rows(cols, tiles, outer, own, inner, count):
    half = own.shape[0]
    return pl.pallas_call(
        first_body,
        out_shape=(
            jax.ShapeDtypeStruct((count * LANES, LANES), jnp.float32),
            jax.ShapeDtypeStruct((3 * half, LANES, LANES), own.dtype),
        ),
        in_specs=[SMEM_SPEC] + [VMEM_SPEC] * 4,
        out_specs=(VMEM_SPEC, VMEM_SPEC),
        compiler_params=PARAMS,
        name="first_rows",
    )(cols, tiles, outer, own, inner)


def more_body(cols_ref, tiles_ref, blocks_ref, out_ref, *, base):
    product_rows(cols_ref, tiles_ref, blocks_ref, out_ref, base)


def more_rows(cols, tiles, blocks, base, count):
    return pl.pallas_call(
        functools.partial(more_body, base=base),
        out_shape=jax.ShapeDtypeStruct((count * LANES, LANES), jnp.float32),
        in_specs=[SMEM_SPEC] + [VMEM_SPEC] * 2,
        out_specs=VMEM_SPEC,
        compiler_params=PARAMS,
        name="more_rows",
    )(cols, tiles, blocks)


def combine_body(*refs, first):
    out_ref, buffer, sem = refs[-3:]
    pairs = (len(refs) - 3) // 2
    start = 0
    for mine_ref, theirs_ref in zip(refs[: 2 * pairs : 2], refs[1 : 2 * pairs : 2]):
        rows = mine_ref.shape[0]
        buffer[start : start + rows, :] = (mine_ref[...] + theirs_ref[...]).astype(buffer.dtype)
        start += rows
    copy = pltpu.make_async_copy(buffer, out_ref.at[pl.ds(first, start)], sem)
    copy.start()
    copy.wait()


def combine(pairs, out, rows, first, dtype):
    parts = [part for pair in pairs for part in pair]
    count, width = sum(mine.shape[0] for mine, _ in pairs), parts[0].shape[1]
    anywhere = pl.BlockSpec(memory_space=pltpu.HBM)
    before = [] if out is None else [out]
    return pl.pallas_call(
        functools.partial(combine_body, first=first),
        out_shape=jax.ShapeDtypeStruct((rows, width), dtype),
        in_specs=[VMEM_SPEC] * len(parts) + [anywhere] * len(before),
        out_specs=anywhere,
        input_output_aliases={len(parts): 0} if before else {},
        scratch_shapes=[pltpu.VMEM((count, width), dtype), pltpu.SemaphoreType.DMA],
        compiler_params=PARAMS,
        name="combine",
    )(*parts, *before)


def per_device(coarse_emb, req_ids, fine_slot, tiles, tile_cols):
    groups, devices = lax.axis_size("grp"), lax.axis_size("dev")
    slots = req_ids.shape[3]
    width = coarse_emb.shape[1]
    row_blocks = tiles.shape[0]
    index = fine_slot.reshape(-1, LANES)
    half = index.shape[0] // 2
    tiles = load(tiles[:, 0])
    asked = lax.all_to_all(
        req_ids.reshape(devices, 1, slots), "dev", split_axis=0, concat_axis=0, tiled=True
    )
    table, first = columns(index, 0, half, coarse_emb)
    wanted = gather(asked, table)
    (second,) = columns(index, half, half)
    received = lax.all_to_all(
        wanted.reshape(devices, slots, width), "dev", split_axis=0, concat_axis=0, tiled=True
    )
    lifted = lift((first, second), received.reshape(devices * slots, width))
    inner = [(i, i ^ 1) for i in range(devices)]
    outer = []
    for g in range(groups):
        outer += [(g * devices + i, g * devices + ((i + 1) ^ 1) - 1) for i in range(1, devices - 1)]
        outer += [(g * devices + i, (g ^ 1) * devices + i) for i in (0, devices - 1)]
    from_outer = lax.ppermute(lifted, ("grp", "dev"), outer).reshape(-1, LANES, width)
    from_inner = lax.ppermute(lifted, "dev", inner).reshape(-1, LANES, width)
    own = lifted.reshape(-1, LANES, width)
    cols = tile_cols[:, 0].T
    parts = []
    base = 0
    for c, count in enumerate(CHUNKS):
        if c == 0:
            mine, blocks = first_rows(cols, tiles, from_outer, own, from_inner, count)
        else:
            mine = more_rows(cols, tiles, blocks, base, count)
        parts.append((mine, lax.ppermute(mine, "grp", [(0, 1), (1, 0)])))
        base += count
    rows = row_blocks * LANES
    out = combine(parts[:-1], None, rows, 0, lifted.dtype)
    return combine(parts[-1:], out, rows, rows - parts[-1][0].shape[0], lifted.dtype)


def solution(mesh):
    return jax.shard_map(
        per_device,
        mesh=mesh,
        in_specs=(
            P("dev", None),
            P("dev", "grp", None, None),
            P("dev", "grp", None),
            P("dev", "grp", None, None, None),
            P("dev", "grp", None),
        ),
        out_specs=P("dev", None),
        check_vma=False,
    )
```

```python
import functools

import jax
import jax.numpy as jnp
from jax import lax
from jax.experimental import pallas as pl
from jax.experimental.pallas import tpu as pltpu
from jax.sharding import PartitionSpec as P


LANES = 128
VMEM_SPEC = pl.BlockSpec(memory_space=pltpu.VMEM)
SMEM_SPEC = pl.BlockSpec(memory_space=pltpu.SMEM)
PARAMS = pltpu.CompilerParams(vmem_limit_bytes=16 * 1024 * 1024)
CHUNKS = (8, 12, 12)


def column_of(index_ref, b):
    return jnp.transpose(jnp.broadcast_to(index_ref[b : b + 1, :], (LANES, LANES)))


def side_by_side(table_ref):
    rows = table_ref.shape[0]
    return jnp.concatenate([table_ref[: rows // 2, :], table_ref[rows // 2 :, :]], axis=1)


def rows_of(wanted, table, depth):
    lane = lax.broadcasted_iota(jnp.int16, (LANES, LANES), 1)
    one = jnp.ones((LANES, LANES), jnp.bfloat16)
    zero = jnp.zeros((LANES, LANES), jnp.bfloat16)
    low = (wanted & (depth - 1)).astype(jnp.int16)
    onehot = jnp.concatenate(
        [jnp.where(low - jnp.int16(c * LANES) == lane, one, zero) for c in range(depth // LANES)],
        axis=1,
    )
    width = table.shape[1] // 2
    found = jnp.dot(onehot, table, preferred_element_type=jnp.float32)
    return jnp.where(wanted >= depth, found[:, width:], found[:, :width])


def gather_body(asked_ref, table_ref, out_ref):
    slots = asked_ref.shape[2]
    each = LANES // slots
    table = table_ref[...]
    row = lax.broadcasted_iota(jnp.int32, (LANES, slots), 0)
    slot = lax.broadcasted_iota(jnp.int32, (LANES, slots), 1)
    chosen = lax.rem(row, slots) == slot
    for b in range(asked_ref.shape[0] // each):
        spread = jnp.concatenate(
            [jnp.broadcast_to(asked_ref[b * each + k], (slots, slots)) for k in range(each)], axis=0
        )
        wanted = jnp.sum(jnp.where(chosen, spread, 0), axis=1, keepdims=True)
        wanted = jnp.broadcast_to(wanted, (LANES, LANES))
        value = rows_of(wanted, table, table_ref.shape[0])
        out_ref[b * LANES : (b + 1) * LANES, :] = value.astype(out_ref.dtype)


def gather(asked, table):
    count = asked.size
    return pl.pallas_call(
        gather_body,
        out_shape=jax.ShapeDtypeStruct((count, table.shape[1] // 2), table.dtype),
        in_specs=[VMEM_SPEC, VMEM_SPEC],
        out_specs=VMEM_SPEC,
        compiler_params=PARAMS,
        name="gather",
    )(asked, table)


def columns_body(index_ref, *refs, first):
    out_ref = refs[-1]
    for b in range(out_ref.shape[0] // LANES):
        out_ref[b * LANES : (b + 1) * LANES, :] = column_of(index_ref, first + b)
    if len(refs) == 3:
        refs[1][...] = side_by_side(refs[0])


def columns(index, first, count, table=None):
    wide = jax.ShapeDtypeStruct((count * LANES, LANES), jnp.int32)
    shapes, arrays = (wide,), (index,)
    if table is not None:
        rows, width = table.shape
        shapes = (jax.ShapeDtypeStruct((rows // 2, 2 * width), table.dtype), wide)
        arrays = (index, table)
    return pl.pallas_call(
        functools.partial(columns_body, first=first),
        out_shape=shapes,
        in_specs=[VMEM_SPEC] * len(arrays),
        out_specs=(VMEM_SPEC,) * len(shapes),
        compiler_params=PARAMS,
        name="columns",
    )(*arrays)


def lift_body(*refs):
    table_ref, out_ref = refs[-2:]
    table = side_by_side(table_ref)
    start = 0
    for wanted_ref in refs[:-2]:
        for b in range(wanted_ref.shape[0] // LANES):
            rows = slice(b * LANES, (b + 1) * LANES)
            value = rows_of(wanted_ref[rows, :], table, table_ref.shape[0] // 2)
            out_ref[start : start + LANES, :] = value.astype(out_ref.dtype)
            start += LANES


def lift(parts, table):
    return pl.pallas_call(
        lift_body,
        out_shape=jax.ShapeDtypeStruct((sum(p.shape[0] for p in parts), table.shape[1]), table.dtype),
        in_specs=[VMEM_SPEC] * (len(parts) + 1),
        out_specs=VMEM_SPEC,
        compiler_params=PARAMS,
        name="lift",
    )(*parts, table)


def load_body(tiles_ref, cols_ref, out_ref, cols_out_ref, sems, *, pieces):
    each = tiles_ref.shape[0] // pieces
    copies = [
        pltpu.make_async_copy(
            tiles_ref.at[pl.ds(p * each, each)], out_ref.at[pl.ds(p * each, each)], sems.at[p]
        )
        for p in range(pieces)
    ]
    copies.append(pltpu.make_async_copy(cols_ref, cols_out_ref, sems.at[pieces]))
    for copy in copies:
        copy.start()
    for copy in copies:
        copy.wait()


def load(tiles, cols):
    return pl.pallas_call(
        functools.partial(load_body, pieces=4),
        out_shape=(pltpu.VMEM(tiles.shape, tiles.dtype), pltpu.SMEM(cols.shape, cols.dtype)),
        in_specs=[pl.BlockSpec(memory_space=pltpu.HBM)] * 2,
        out_specs=(VMEM_SPEC, SMEM_SPEC),
        scratch_shapes=[pltpu.SemaphoreType.DMA((5,))],
        compiler_params=pltpu.CompilerParams(vmem_limit_bytes=48 * 1024 * 1024),
        name="load",
    )(tiles, cols)


def product_rows(cols_ref, tiles_ref, blocks_ref, out_ref, base):
    per_row = tiles_ref.shape[1]
    half = blocks_ref.shape[0] // 3
    count = out_ref.shape[0] // LANES
    group = lax.axis_index("grp").astype(jnp.int32)

    for i in range(count):
        r = base + i
        left = jnp.concatenate([tiles_ref[r, t] for t in range(per_row)], axis=1)
        right = jnp.concatenate([blocks_ref[cols_ref[t, r]] for t in range(per_row)], axis=0)
        product = jnp.dot(left, right, preferred_element_type=jnp.float32)
        own = blocks_ref[half + r % half].astype(jnp.float32)
        own = jnp.where(group == r // half, own, 0.0)
        out_ref[i * LANES : (i + 1) * LANES, :] = own - 0.5 * product


def first_body(cols_ref, tiles_ref, outer_ref, own_ref, inner_ref, out_ref, blocks_ref):
    half = own_ref.shape[0]
    place = lax.axis_index("dev")
    odd = lax.rem(place, 2) == 1
    ends = (place == 0) | (place == lax.axis_size("dev") - 1)
    outer = jnp.where(ends, jnp.zeros(own_ref.shape, own_ref.dtype), outer_ref[...])
    blocks_ref[half : 2 * half] = own_ref[...]
    blocks_ref[pl.ds(jnp.where(odd, 2 * half, 0), half)] = outer
    blocks_ref[pl.ds(jnp.where(odd, 0, 2 * half), half)] = inner_ref[...]
    product_rows(cols_ref, tiles_ref, blocks_ref, out_ref, 0)


def first_rows(cols, tiles, outer, own, inner, count):
    half = own.shape[0]
    return pl.pallas_call(
        first_body,
        out_shape=(
            jax.ShapeDtypeStruct((count * LANES, LANES), jnp.float32),
            jax.ShapeDtypeStruct((3 * half, LANES, LANES), own.dtype),
        ),
        in_specs=[SMEM_SPEC] + [VMEM_SPEC] * 4,
        out_specs=(VMEM_SPEC, VMEM_SPEC),
        compiler_params=PARAMS,
        name="first_rows",
    )(cols, tiles, outer, own, inner)


def more_body(cols_ref, tiles_ref, blocks_ref, out_ref, *, base):
    product_rows(cols_ref, tiles_ref, blocks_ref, out_ref, base)


def more_rows(cols, tiles, blocks, base, count):
    return pl.pallas_call(
        functools.partial(more_body, base=base),
        out_shape=jax.ShapeDtypeStruct((count * LANES, LANES), jnp.float32),
        in_specs=[SMEM_SPEC] + [VMEM_SPEC] * 2,
        out_specs=VMEM_SPEC,
        compiler_params=PARAMS,
        name="more_rows",
    )(cols, tiles, blocks)


def combine_body(*refs, first):
    out_ref, buffer, sem = refs[-3:]
    pairs = (len(refs) - 3) // 2
    start = 0
    for mine_ref, theirs_ref in zip(refs[: 2 * pairs : 2], refs[1 : 2 * pairs : 2]):
        rows = mine_ref.shape[0]
        buffer[start : start + rows, :] = (mine_ref[...] + theirs_ref[...]).astype(buffer.dtype)
        start += rows
    copy = pltpu.make_async_copy(buffer, out_ref.at[pl.ds(first, start)], sem)
    copy.start()
    copy.wait()


def combine(pairs, out, rows, first, dtype):
    parts = [part for pair in pairs for part in pair]
    count, width = sum(mine.shape[0] for mine, _ in pairs), parts[0].shape[1]
    anywhere = pl.BlockSpec(memory_space=pltpu.HBM)
    before = [] if out is None else [out]
    return pl.pallas_call(
        functools.partial(combine_body, first=first),
        out_shape=jax.ShapeDtypeStruct((rows, width), dtype),
        in_specs=[VMEM_SPEC] * len(parts) + [anywhere] * len(before),
        out_specs=anywhere,
        input_output_aliases={len(parts): 0} if before else {},
        scratch_shapes=[pltpu.VMEM((count, width), dtype), pltpu.SemaphoreType.DMA],
        compiler_params=PARAMS,
        name="combine",
    )(*parts, *before)


def per_device(coarse_emb, req_ids, fine_slot, tiles, tile_cols):
    groups, devices = lax.axis_size("grp"), lax.axis_size("dev")
    slots = req_ids.shape[3]
    width = coarse_emb.shape[1]
    row_blocks = tiles.shape[0]
    index = fine_slot.reshape(-1, LANES)
    half = index.shape[0] // 2
    tiles, cols = load(tiles[:, 0], tile_cols[:, 0].T)
    asked = lax.all_to_all(
        req_ids.reshape(devices, 1, slots), "dev", split_axis=0, concat_axis=0, tiled=True
    )
    table, first = columns(index, 0, half, coarse_emb)
    wanted = gather(asked, table)
    (second,) = columns(index, half, half)
    received = lax.all_to_all(
        wanted.reshape(devices, slots, width), "dev", split_axis=0, concat_axis=0, tiled=True
    )
    lifted = lift((first, second), received.reshape(devices * slots, width))
    inner = [(i, i ^ 1) for i in range(devices)]
    outer = []
    for g in range(groups):
        outer += [(g * devices + i, g * devices + ((i + 1) ^ 1) - 1) for i in range(1, devices - 1)]
        outer += [(g * devices + i, (g ^ 1) * devices + i) for i in (0, devices - 1)]
    from_outer = lax.ppermute(lifted, ("grp", "dev"), outer).reshape(-1, LANES, width)
    from_inner = lax.ppermute(lifted, "dev", inner).reshape(-1, LANES, width)
    own = lifted.reshape(-1, LANES, width)
    parts = []
    base = 0
    for c, count in enumerate(CHUNKS):
        if c == 0:
            mine, blocks = first_rows(cols, tiles, from_outer, own, from_inner, count)
        else:
            mine = more_rows(cols, tiles, blocks, base, count)
        parts.append((mine, lax.ppermute(mine, "grp", [(0, 1), (1, 0)])))
        base += count
    rows = row_blocks * LANES
    out, base = None, 0
    for part in parts:
        out = combine([part], out, rows, base, lifted.dtype)
        base += part[0].shape[0]
    return out


def solution(mesh):
    return jax.shard_map(
        per_device,
        mesh=mesh,
        in_specs=(
            P("dev", None),
            P("dev", "grp", None, None),
            P("dev", "grp", None),
            P("dev", "grp", None, None, None),
            P("dev", "grp", None),
        ),
        out_specs=P("dev", None),
        check_vma=False,
    )
```

```python
import functools

import jax
import jax.numpy as jnp
from jax import lax
from jax.experimental import pallas as pl
from jax.experimental.pallas import tpu as pltpu
from jax.sharding import PartitionSpec as P


LANES = 128
VMEM_SPEC = pl.BlockSpec(memory_space=pltpu.VMEM)
SMEM_SPEC = pl.BlockSpec(memory_space=pltpu.SMEM)
PARAMS = pltpu.CompilerParams(vmem_limit_bytes=16 * 1024 * 1024)
CHUNKS = (8, 12, 12)


def column_of(index_ref, b):
    return jnp.transpose(jnp.broadcast_to(index_ref[b : b + 1, :], (LANES, LANES)))


def side_by_side(table_ref):
    rows = table_ref.shape[0]
    return jnp.concatenate([table_ref[: rows // 2, :], table_ref[rows // 2 :, :]], axis=1)


def rows_of(wanted, table, depth):
    lane = lax.broadcasted_iota(jnp.int16, (LANES, LANES), 1)
    one = jnp.ones((LANES, LANES), jnp.bfloat16)
    zero = jnp.zeros((LANES, LANES), jnp.bfloat16)
    low = (wanted & (depth - 1)).astype(jnp.int16)
    onehot = jnp.concatenate(
        [jnp.where(low - jnp.int16(c * LANES) == lane, one, zero) for c in range(depth // LANES)],
        axis=1,
    )
    width = table.shape[1] // 2
    found = jnp.dot(onehot, table, preferred_element_type=jnp.float32)
    return jnp.where(wanted >= depth, found[:, width:], found[:, :width])


def gather_body(asked_ref, table_ref, out_ref):
    slots = asked_ref.shape[2]
    each = LANES // slots
    table = table_ref[...]
    row = lax.broadcasted_iota(jnp.int32, (LANES, slots), 0)
    slot = lax.broadcasted_iota(jnp.int32, (LANES, slots), 1)
    chosen = lax.rem(row, slots) == slot
    for b in range(asked_ref.shape[0] // each):
        spread = jnp.concatenate(
            [jnp.broadcast_to(asked_ref[b * each + k], (slots, slots)) for k in range(each)], axis=0
        )
        wanted = jnp.sum(jnp.where(chosen, spread, 0), axis=1, keepdims=True)
        wanted = jnp.broadcast_to(wanted, (LANES, LANES))
        value = rows_of(wanted, table, table_ref.shape[0])
        out_ref[b * LANES : (b + 1) * LANES, :] = value.astype(out_ref.dtype)


def gather(asked, table):
    count = asked.size
    return pl.pallas_call(
        gather_body,
        out_shape=jax.ShapeDtypeStruct((count, table.shape[1] // 2), table.dtype),
        in_specs=[VMEM_SPEC, VMEM_SPEC],
        out_specs=VMEM_SPEC,
        compiler_params=PARAMS,
        name="gather",
    )(asked, table)


def columns_body(index_ref, *refs, first):
    out_ref = refs[-1]
    for b in range(out_ref.shape[0] // LANES):
        out_ref[b * LANES : (b + 1) * LANES, :] = column_of(index_ref, first + b)
    if len(refs) == 3:
        refs[1][...] = side_by_side(refs[0])


def columns(index, first, count, table=None):
    wide = jax.ShapeDtypeStruct((count * LANES, LANES), jnp.int32)
    shapes, arrays = (wide,), (index,)
    if table is not None:
        rows, width = table.shape
        shapes = (jax.ShapeDtypeStruct((rows // 2, 2 * width), table.dtype), wide)
        arrays = (index, table)
    return pl.pallas_call(
        functools.partial(columns_body, first=first),
        out_shape=shapes,
        in_specs=[VMEM_SPEC] * len(arrays),
        out_specs=(VMEM_SPEC,) * len(shapes),
        compiler_params=PARAMS,
        name="columns",
    )(*arrays)


def lift_body(*refs):
    table_ref, out_ref = refs[-2:]
    table = side_by_side(table_ref)
    start = 0
    for wanted_ref in refs[:-2]:
        for b in range(wanted_ref.shape[0] // LANES):
            rows = slice(b * LANES, (b + 1) * LANES)
            value = rows_of(wanted_ref[rows, :], table, table_ref.shape[0] // 2)
            out_ref[start : start + LANES, :] = value.astype(out_ref.dtype)
            start += LANES


def lift(parts, table):
    return pl.pallas_call(
        lift_body,
        out_shape=jax.ShapeDtypeStruct((sum(p.shape[0] for p in parts), table.shape[1]), table.dtype),
        in_specs=[VMEM_SPEC] * (len(parts) + 1),
        out_specs=VMEM_SPEC,
        compiler_params=PARAMS,
        name="lift",
    )(*parts, table)


def load_body(tiles_ref, cols_ref, out_ref, cols_out_ref, sems, *, pieces):
    each = tiles_ref.shape[0] // pieces
    copies = [
        pltpu.make_async_copy(
            tiles_ref.at[pl.ds(p * each, each)], out_ref.at[pl.ds(p * each, each)], sems.at[p]
        )
        for p in range(pieces)
    ]
    copies.append(pltpu.make_async_copy(cols_ref, cols_out_ref, sems.at[pieces]))
    for copy in copies:
        copy.start()
    for copy in copies:
        copy.wait()


def load(tiles, cols):
    return pl.pallas_call(
        functools.partial(load_body, pieces=4),
        out_shape=(pltpu.VMEM(tiles.shape, tiles.dtype), pltpu.SMEM(cols.shape, cols.dtype)),
        in_specs=[pl.BlockSpec(memory_space=pltpu.HBM)] * 2,
        out_specs=(VMEM_SPEC, SMEM_SPEC),
        scratch_shapes=[pltpu.SemaphoreType.DMA((5,))],
        compiler_params=pltpu.CompilerParams(vmem_limit_bytes=48 * 1024 * 1024),
        name="load",
    )(tiles, cols)


def product_rows(cols_ref, tiles_ref, blocks_ref, out_ref, base):
    per_row = tiles_ref.shape[1]
    half = blocks_ref.shape[0] // 3
    count = out_ref.shape[0] // LANES
    group = lax.axis_index("grp").astype(jnp.int32)

    for i in range(count):
        r = base + i
        left = jnp.concatenate([tiles_ref[r, t] for t in range(per_row)], axis=1)
        right = jnp.concatenate([blocks_ref[cols_ref[t, r]] for t in range(per_row)], axis=0)
        product = jnp.dot(left, right, preferred_element_type=jnp.float32)
        own = blocks_ref[half + r % half].astype(jnp.float32)
        own = jnp.where(group == r // half, own, 0.0)
        out_ref[i * LANES : (i + 1) * LANES, :] = own - 0.5 * product


def first_body(cols_ref, tiles_ref, outer_ref, own_ref, inner_ref, out_ref, blocks_ref):
    half = own_ref.shape[0]
    place = lax.axis_index("dev")
    odd = lax.rem(place, 2) == 1
    ends = (place == 0) | (place == lax.axis_size("dev") - 1)
    outer = jnp.where(ends, jnp.zeros(own_ref.shape, own_ref.dtype), outer_ref[...])
    blocks_ref[half : 2 * half] = own_ref[...]
    blocks_ref[pl.ds(jnp.where(odd, 2 * half, 0), half)] = outer
    blocks_ref[pl.ds(jnp.where(odd, 0, 2 * half), half)] = inner_ref[...]
    product_rows(cols_ref, tiles_ref, blocks_ref, out_ref, 0)


def first_rows(cols, tiles, outer, own, inner, count):
    half = own.shape[0]
    return pl.pallas_call(
        first_body,
        out_shape=(
            jax.ShapeDtypeStruct((count * LANES, LANES), jnp.float32),
            jax.ShapeDtypeStruct((3 * half, LANES, LANES), own.dtype),
        ),
        in_specs=[SMEM_SPEC] + [VMEM_SPEC] * 4,
        out_specs=(VMEM_SPEC, VMEM_SPEC),
        compiler_params=PARAMS,
        name="first_rows",
    )(cols, tiles, outer, own, inner)


def more_body(cols_ref, tiles_ref, blocks_ref, out_ref, *, base):
    product_rows(cols_ref, tiles_ref, blocks_ref, out_ref, base)


def more_rows(cols, tiles, blocks, base, count):
    return pl.pallas_call(
        functools.partial(more_body, base=base),
        out_shape=jax.ShapeDtypeStruct((count * LANES, LANES), jnp.float32),
        in_specs=[SMEM_SPEC] + [VMEM_SPEC] * 2,
        out_specs=VMEM_SPEC,
        compiler_params=PARAMS,
        name="more_rows",
    )(cols, tiles, blocks)


def combine_body(*refs, first):
    out_ref, buffer, sem = refs[-3:]
    pairs = (len(refs) - 3) // 2
    start = 0
    for mine_ref, theirs_ref in zip(refs[: 2 * pairs : 2], refs[1 : 2 * pairs : 2]):
        rows = mine_ref.shape[0]
        buffer[start : start + rows, :] = (mine_ref[...] + theirs_ref[...]).astype(buffer.dtype)
        start += rows
    copy = pltpu.make_async_copy(buffer, out_ref.at[pl.ds(first, start)], sem)
    copy.start()
    copy.wait()


def combine(pairs, out, rows, first, dtype):
    parts = [part for pair in pairs for part in pair]
    count, width = sum(mine.shape[0] for mine, _ in pairs), parts[0].shape[1]
    anywhere = pl.BlockSpec(memory_space=pltpu.HBM)
    before = [] if out is None else [out]
    return pl.pallas_call(
        functools.partial(combine_body, first=first),
        out_shape=jax.ShapeDtypeStruct((rows, width), dtype),
        in_specs=[VMEM_SPEC] * len(parts) + [anywhere] * len(before),
        out_specs=anywhere,
        input_output_aliases={len(parts): 0} if before else {},
        scratch_shapes=[pltpu.VMEM((count, width), dtype), pltpu.SemaphoreType.DMA],
        compiler_params=PARAMS,
        name="combine",
    )(*parts, *before)


def per_device(coarse_emb, req_ids, fine_slot, tiles, tile_cols):
    groups, devices = lax.axis_size("grp"), lax.axis_size("dev")
    slots = req_ids.shape[3]
    width = coarse_emb.shape[1]
    row_blocks = tiles.shape[0]
    index = fine_slot.reshape(-1, LANES)
    half = index.shape[0] // 2
    tiles, cols = load(tiles[:, 0], tile_cols[:, 0].T)
    asked = lax.all_to_all(
        req_ids.reshape(devices, 1, slots), "dev", split_axis=0, concat_axis=0, tiled=True
    )
    table, first = columns(index, 0, 2 * half, coarse_emb)
    wanted = gather(asked, table)
    received = lax.all_to_all(
        wanted.reshape(devices, slots, width), "dev", split_axis=0, concat_axis=0, tiled=True
    )
    lifted = lift((first,), received.reshape(devices * slots, width))
    inner = [(i, i ^ 1) for i in range(devices)]
    outer = []
    for g in range(groups):
        outer += [(g * devices + i, g * devices + ((i + 1) ^ 1) - 1) for i in range(1, devices - 1)]
        outer += [(g * devices + i, (g ^ 1) * devices + i) for i in (0, devices - 1)]
    from_outer = lax.ppermute(lifted, ("grp", "dev"), outer).reshape(-1, LANES, width)
    from_inner = lax.ppermute(lifted, "dev", inner).reshape(-1, LANES, width)
    own = lifted.reshape(-1, LANES, width)
    parts = []
    base = 0
    for c, count in enumerate(CHUNKS):
        if c == 0:
            mine, blocks = first_rows(cols, tiles, from_outer, own, from_inner, count)
        else:
            mine = more_rows(cols, tiles, blocks, base, count)
        parts.append((mine, lax.ppermute(mine, "grp", [(0, 1), (1, 0)])))
        base += count
    rows = row_blocks * LANES
    out, base = None, 0
    for part in parts:
        out = combine([part], out, rows, base, lifted.dtype)
        base += part[0].shape[0]
    return out


def solution(mesh):
    return jax.shard_map(
        per_device,
        mesh=mesh,
        in_specs=(
            P("dev", None),
            P("dev", "grp", None, None),
            P("dev", "grp", None),
            P("dev", "grp", None, None, None),
            P("dev", "grp", None),
        ),
        out_specs=P("dev", None),
        check_vma=False,
    )
```

```python
import functools

import jax
import jax.numpy as jnp
from jax import lax
from jax.experimental import pallas as pl
from jax.experimental.pallas import tpu as pltpu
from jax.sharding import PartitionSpec as P


LANES = 128
VMEM_SPEC = pl.BlockSpec(memory_space=pltpu.VMEM)
SMEM_SPEC = pl.BlockSpec(memory_space=pltpu.SMEM)
PARAMS = pltpu.CompilerParams(vmem_limit_bytes=16 * 1024 * 1024)
CHUNKS = (8, 12, 12)


def column_of(index_ref, b):
    return jnp.transpose(jnp.broadcast_to(index_ref[b : b + 1, :], (LANES, LANES)))


def side_by_side(table_ref):
    rows = table_ref.shape[0]
    return jnp.concatenate([table_ref[: rows // 2, :], table_ref[rows // 2 :, :]], axis=1)


def rows_of(wanted, table, depth):
    lane = lax.broadcasted_iota(jnp.int16, (LANES, LANES), 1)
    one = jnp.ones((LANES, LANES), jnp.bfloat16)
    zero = jnp.zeros((LANES, LANES), jnp.bfloat16)
    low = (wanted & (depth - 1)).astype(jnp.int16)
    onehot = jnp.concatenate(
        [jnp.where(low - jnp.int16(c * LANES) == lane, one, zero) for c in range(depth // LANES)],
        axis=1,
    )
    width = table.shape[1] // 2
    found = jnp.dot(onehot, table, preferred_element_type=jnp.float32)
    return jnp.where(wanted >= depth, found[:, width:], found[:, :width])


def start_body(
    lists_ref, table_ref, index_ref, lists_out, table_out, index_out, lists_buffer, table_buffer, sems
):
    copies = [
        pltpu.make_async_copy(lists_ref, lists_buffer, sems.at[0]),
        pltpu.make_async_copy(table_ref, table_buffer, sems.at[1]),
        pltpu.make_async_copy(index_ref, index_out, sems.at[2]),
    ]
    for copy in copies:
        copy.start()
    copies[0].wait()
    slots, owners = lists_ref.shape
    filled = jnp.concatenate([lists_buffer[...]] * (owners // slots), axis=0)
    lists_out[...] = jnp.transpose(filled)[:, :slots]
    copies[1].wait()
    table_out[...] = side_by_side(table_buffer)
    copies[2].wait()


def start(lists, table, index):
    rows, width = table.shape
    return pl.pallas_call(
        start_body,
        out_shape=(
            pltpu.VMEM(lists.shape[::-1], lists.dtype),
            pltpu.VMEM((rows // 2, 2 * width), table.dtype),
            pltpu.VMEM(index.shape, index.dtype),
        ),
        in_specs=[pl.BlockSpec(memory_space=pltpu.HBM)] * 3,
        out_specs=(VMEM_SPEC,) * 3,
        scratch_shapes=[
            pltpu.VMEM(lists.shape, lists.dtype),
            pltpu.VMEM(table.shape, table.dtype),
            pltpu.SemaphoreType.DMA((3,)),
        ],
        compiler_params=pltpu.CompilerParams(vmem_limit_bytes=56 * 1024 * 1024),
        name="start",
    )(lists, table, index)


def gather_body(asked_ref, table_ref, out_ref):
    slots = asked_ref.shape[2]
    each = LANES // slots
    table = table_ref[...]
    row = lax.broadcasted_iota(jnp.int32, (LANES, slots), 0)
    slot = lax.broadcasted_iota(jnp.int32, (LANES, slots), 1)
    chosen = lax.rem(row, slots) == slot
    for b in range(asked_ref.shape[0] // each):
        spread = jnp.concatenate(
            [jnp.broadcast_to(asked_ref[b * each + k], (slots, slots)) for k in range(each)], axis=0
        )
        wanted = jnp.sum(jnp.where(chosen, spread, 0), axis=1, keepdims=True)
        wanted = jnp.broadcast_to(wanted, (LANES, LANES))
        value = rows_of(wanted, table, table_ref.shape[0])
        out_ref[b * LANES : (b + 1) * LANES, :] = value.astype(out_ref.dtype)


def gather(asked, table):
    return pl.pallas_call(
        gather_body,
        out_shape=jax.ShapeDtypeStruct((asked.size, table.shape[1] // 2), table.dtype),
        in_specs=[VMEM_SPEC, VMEM_SPEC],
        out_specs=VMEM_SPEC,
        compiler_params=PARAMS,
        name="gather",
    )(asked, table)


def lift_body(index_ref, table_ref, out_ref):
    table = side_by_side(table_ref)
    for b in range(index_ref.shape[0]):
        value = rows_of(column_of(index_ref, b), table, table_ref.shape[0] // 2)
        out_ref[b * LANES : (b + 1) * LANES, :] = value.astype(out_ref.dtype)


def lift(index, table):
    return pl.pallas_call(
        lift_body,
        out_shape=jax.ShapeDtypeStruct((index.size, table.shape[1]), table.dtype),
        in_specs=[VMEM_SPEC, VMEM_SPEC],
        out_specs=VMEM_SPEC,
        compiler_params=PARAMS,
        name="lift",
    )(index, table)


def load_body(tiles_ref, cols_ref, out_ref, cols_out_ref, sems, *, pieces):
    each = tiles_ref.shape[0] // pieces
    copies = [
        pltpu.make_async_copy(
            tiles_ref.at[pl.ds(p * each, each)], out_ref.at[pl.ds(p * each, each)], sems.at[p]
        )
        for p in range(pieces)
    ]
    copies.append(pltpu.make_async_copy(cols_ref, cols_out_ref, sems.at[pieces]))
    for copy in copies:
        copy.start()
    for copy in copies:
        copy.wait()


def load(tiles, cols):
    return pl.pallas_call(
        functools.partial(load_body, pieces=4),
        out_shape=(pltpu.VMEM(tiles.shape, tiles.dtype), pltpu.SMEM(cols.shape, cols.dtype)),
        in_specs=[pl.BlockSpec(memory_space=pltpu.HBM)] * 2,
        out_specs=(VMEM_SPEC, SMEM_SPEC),
        scratch_shapes=[pltpu.SemaphoreType.DMA((5,))],
        compiler_params=pltpu.CompilerParams(vmem_limit_bytes=48 * 1024 * 1024),
        name="load",
    )(tiles, cols)


def product_rows(cols_ref, tiles_ref, blocks_ref, out_ref, base):
    per_row = tiles_ref.shape[1]
    half = blocks_ref.shape[0] // 3
    count = out_ref.shape[0] // LANES
    group = lax.axis_index("grp").astype(jnp.int32)

    for i in range(count):
        r = base + i
        left = jnp.concatenate([tiles_ref[r, t] for t in range(per_row)], axis=1)
        right = jnp.concatenate([blocks_ref[cols_ref[t, r]] for t in range(per_row)], axis=0)
        product = jnp.dot(left, right, preferred_element_type=jnp.float32)
        own = blocks_ref[half + r % half].astype(jnp.float32)
        own = jnp.where(group == r // half, own, 0.0)
        out_ref[i * LANES : (i + 1) * LANES, :] = own - 0.5 * product


def first_body(cols_ref, tiles_ref, outer_ref, own_ref, inner_ref, out_ref, blocks_ref):
    half = own_ref.shape[0]
    place = lax.axis_index("dev")
    odd = lax.rem(place, 2) == 1
    ends = (place == 0) | (place == lax.axis_size("dev") - 1)
    outer = jnp.where(ends, jnp.zeros(own_ref.shape, own_ref.dtype), outer_ref[...])
    blocks_ref[half : 2 * half] = own_ref[...]
    blocks_ref[pl.ds(jnp.where(odd, 2 * half, 0), half)] = outer
    blocks_ref[pl.ds(jnp.where(odd, 0, 2 * half), half)] = inner_ref[...]
    product_rows(cols_ref, tiles_ref, blocks_ref, out_ref, 0)


def first_rows(cols, tiles, outer, own, inner, count):
    half = own.shape[0]
    return pl.pallas_call(
        first_body,
        out_shape=(
            jax.ShapeDtypeStruct((count * LANES, LANES), jnp.float32),
            jax.ShapeDtypeStruct((3 * half, LANES, LANES), own.dtype),
        ),
        in_specs=[SMEM_SPEC] + [VMEM_SPEC] * 4,
        out_specs=(VMEM_SPEC, VMEM_SPEC),
        compiler_params=PARAMS,
        name="first_rows",
    )(cols, tiles, outer, own, inner)


def more_body(cols_ref, tiles_ref, blocks_ref, out_ref, *, base):
    product_rows(cols_ref, tiles_ref, blocks_ref, out_ref, base)


def more_rows(cols, tiles, blocks, base, count):
    return pl.pallas_call(
        functools.partial(more_body, base=base),
        out_shape=jax.ShapeDtypeStruct((count * LANES, LANES), jnp.float32),
        in_specs=[SMEM_SPEC] + [VMEM_SPEC] * 2,
        out_specs=VMEM_SPEC,
        compiler_params=PARAMS,
        name="more_rows",
    )(cols, tiles, blocks)


def combine_body(*refs, first):
    out_ref, buffer, sem = refs[-3:]
    pairs = (len(refs) - 3) // 2
    start = 0
    for mine_ref, theirs_ref in zip(refs[: 2 * pairs : 2], refs[1 : 2 * pairs : 2]):
        rows = mine_ref.shape[0]
        buffer[start : start + rows, :] = (mine_ref[...] + theirs_ref[...]).astype(buffer.dtype)
        start += rows
    copy = pltpu.make_async_copy(buffer, out_ref.at[pl.ds(first, start)], sem)
    copy.start()
    copy.wait()


def combine(pairs, out, rows, first, dtype):
    parts = [part for pair in pairs for part in pair]
    count, width = sum(mine.shape[0] for mine, _ in pairs), parts[0].shape[1]
    anywhere = pl.BlockSpec(memory_space=pltpu.HBM)
    before = [] if out is None else [out]
    return pl.pallas_call(
        functools.partial(combine_body, first=first),
        out_shape=jax.ShapeDtypeStruct((rows, width), dtype),
        in_specs=[VMEM_SPEC] * len(parts) + [anywhere] * len(before),
        out_specs=anywhere,
        input_output_aliases={len(parts): 0} if before else {},
        scratch_shapes=[pltpu.VMEM((count, width), dtype), pltpu.SemaphoreType.DMA],
        compiler_params=PARAMS,
        name="combine",
    )(*parts, *before)


def per_device(coarse_emb, req_ids, fine_slot, tiles, tile_cols):
    groups, devices = lax.axis_size("grp"), lax.axis_size("dev")
    slots = req_ids.shape[3]
    width = coarse_emb.shape[1]
    row_blocks = tiles.shape[0]
    lists, table, index = start(req_ids[0, 0].T, coarse_emb, fine_slot.reshape(-1, LANES))
    tiles, cols = load(tiles[:, 0], tile_cols[:, 0].T)
    asked = lax.all_to_all(
        lists.reshape(devices, 1, slots), "dev", split_axis=0, concat_axis=0, tiled=True
    )
    wanted = gather(asked, table)
    received = lax.all_to_all(
        wanted.reshape(devices, slots, width), "dev", split_axis=0, concat_axis=0, tiled=True
    )
    lifted = lift(index, received.reshape(devices * slots, width))
    inner = [(i, i ^ 1) for i in range(devices)]
    outer = []
    for g in range(groups):
        outer += [(g * devices + i, g * devices + ((i + 1) ^ 1) - 1) for i in range(1, devices - 1)]
        outer += [(g * devices + i, (g ^ 1) * devices + i) for i in (0, devices - 1)]
    from_outer = lax.ppermute(lifted, ("grp", "dev"), outer).reshape(-1, LANES, width)
    from_inner = lax.ppermute(lifted, "dev", inner).reshape(-1, LANES, width)
    own = lifted.reshape(-1, LANES, width)
    parts = []
    base = 0
    for c, count in enumerate(CHUNKS):
        if c == 0:
            mine, blocks = first_rows(cols, tiles, from_outer, own, from_inner, count)
        else:
            mine = more_rows(cols, tiles, blocks, base, count)
        parts.append((mine, lax.ppermute(mine, "grp", [(0, 1), (1, 0)])))
        base += count
    rows = row_blocks * LANES
    out, base = None, 0
    for part in parts:
        out = combine([part], out, rows, base, lifted.dtype)
        base += part[0].shape[0]
    return out


def solution(mesh):
    return jax.shard_map(
        per_device,
        mesh=mesh,
        in_specs=(
            P("dev", None),
            P("dev", "grp", None, None),
            P("dev", "grp", None),
            P("dev", "grp", None, None, None),
            P("dev", "grp", None),
        ),
        out_specs=P("dev", None),
        check_vma=False,
    )
```

```python
import functools

import jax
import jax.numpy as jnp
from jax import lax
from jax.experimental import pallas as pl
from jax.experimental.pallas import tpu as pltpu
from jax.sharding import PartitionSpec as P


LANES = 128
VMEM_SPEC = pl.BlockSpec(memory_space=pltpu.VMEM)
SMEM_SPEC = pl.BlockSpec(memory_space=pltpu.SMEM)
PARAMS = pltpu.CompilerParams(vmem_limit_bytes=16 * 1024 * 1024)
CHUNKS = (8, 16, 8)
PIECES = 4


def column_of(index_ref, b):
    return jnp.transpose(jnp.broadcast_to(index_ref[b : b + 1, :], (LANES, LANES)))


def side_by_side(table_ref):
    rows = table_ref.shape[0]
    return jnp.concatenate([table_ref[: rows // 2, :], table_ref[rows // 2 :, :]], axis=1)


def rows_of(wanted, table, depth):
    lane = lax.broadcasted_iota(jnp.int16, (LANES, LANES), 1)
    one = jnp.ones((LANES, LANES), jnp.bfloat16)
    zero = jnp.zeros((LANES, LANES), jnp.bfloat16)
    low = (wanted & (depth - 1)).astype(jnp.int16)
    onehot = jnp.concatenate(
        [jnp.where(low - jnp.int16(c * LANES) == lane, one, zero) for c in range(depth // LANES)],
        axis=1,
    )
    width = table.shape[1] // 2
    found = jnp.dot(onehot, table, preferred_element_type=jnp.float32)
    return jnp.where(wanted >= depth, found[:, width:], found[:, :width])


def start_body(
    lists_ref, table_ref, index_ref, lists_out, table_out, index_out, lists_buffer, table_buffer, sems
):
    copies = [
        pltpu.make_async_copy(lists_ref, lists_buffer, sems.at[0]),
        pltpu.make_async_copy(table_ref, table_buffer, sems.at[1]),
        pltpu.make_async_copy(index_ref, index_out, sems.at[2]),
    ]
    for copy in copies:
        copy.start()
    copies[0].wait()
    slots, owners = lists_ref.shape
    filled = jnp.concatenate([lists_buffer[...]] * (owners // slots), axis=0)
    lists_out[...] = jnp.transpose(filled)[:, :slots]
    copies[1].wait()
    table_out[...] = side_by_side(table_buffer)
    copies[2].wait()


def start(lists, table, index):
    rows, width = table.shape
    return pl.pallas_call(
        start_body,
        out_shape=(
            pltpu.VMEM(lists.shape[::-1], lists.dtype),
            pltpu.VMEM((rows // 2, 2 * width), table.dtype),
            pltpu.VMEM(index.shape, index.dtype),
        ),
        in_specs=[pl.BlockSpec(memory_space=pltpu.HBM)] * 3,
        out_specs=(VMEM_SPEC,) * 3,
        scratch_shapes=[
            pltpu.VMEM(lists.shape, lists.dtype),
            pltpu.VMEM(table.shape, table.dtype),
            pltpu.SemaphoreType.DMA((3,)),
        ],
        compiler_params=pltpu.CompilerParams(vmem_limit_bytes=56 * 1024 * 1024),
        name="start",
    )(lists, table, index)


def gather_body(asked_ref, table_ref, out_ref):
    slots = asked_ref.shape[2]
    each = LANES // slots
    table = table_ref[...]
    row = lax.broadcasted_iota(jnp.int32, (LANES, slots), 0)
    slot = lax.broadcasted_iota(jnp.int32, (LANES, slots), 1)
    chosen = lax.rem(row, slots) == slot
    for b in range(asked_ref.shape[0] // each):
        spread = jnp.concatenate(
            [jnp.broadcast_to(asked_ref[b * each + k], (slots, slots)) for k in range(each)], axis=0
        )
        wanted = jnp.sum(jnp.where(chosen, spread, 0), axis=1, keepdims=True)
        wanted = jnp.broadcast_to(wanted, (LANES, LANES))
        value = rows_of(wanted, table, table_ref.shape[0])
        out_ref[b * LANES : (b + 1) * LANES, :] = value.astype(out_ref.dtype)


def gather(asked, table):
    return pl.pallas_call(
        gather_body,
        out_shape=jax.ShapeDtypeStruct((asked.size, table.shape[1] // 2), table.dtype),
        in_specs=[VMEM_SPEC, VMEM_SPEC],
        out_specs=VMEM_SPEC,
        compiler_params=PARAMS,
        name="gather",
    )(asked, table)


def lift_body(index_ref, table_ref, out_ref):
    table = side_by_side(table_ref)
    for b in range(index_ref.shape[0]):
        value = rows_of(column_of(index_ref, b), table, table_ref.shape[0] // 2)
        out_ref[b * LANES : (b + 1) * LANES, :] = value.astype(out_ref.dtype)


def lift(index, table):
    return pl.pallas_call(
        lift_body,
        out_shape=jax.ShapeDtypeStruct((index.size, table.shape[1]), table.dtype),
        in_specs=[VMEM_SPEC, VMEM_SPEC],
        out_specs=VMEM_SPEC,
        compiler_params=PARAMS,
        name="lift",
    )(index, table)


def load_body(tiles_ref, cols_ref, out_ref, cols_out_ref, sems, *, pieces):
    each = tiles_ref.shape[0] // pieces
    copies = [
        pltpu.make_async_copy(
            tiles_ref.at[pl.ds(p * each, each)], out_ref.at[pl.ds(p * each, each)], sems.at[p]
        )
        for p in range(pieces)
    ]
    copies.append(pltpu.make_async_copy(cols_ref, cols_out_ref, sems.at[pieces]))
    for copy in copies:
        copy.start()
    for copy in copies:
        copy.wait()


def load(tiles, cols):
    return pl.pallas_call(
        functools.partial(load_body, pieces=4),
        out_shape=(pltpu.VMEM(tiles.shape, tiles.dtype), pltpu.SMEM(cols.shape, cols.dtype)),
        in_specs=[pl.BlockSpec(memory_space=pltpu.HBM)] * 2,
        out_specs=(VMEM_SPEC, SMEM_SPEC),
        scratch_shapes=[pltpu.SemaphoreType.DMA((5,))],
        compiler_params=pltpu.CompilerParams(vmem_limit_bytes=48 * 1024 * 1024),
        name="load",
    )(tiles, cols)


def product_rows(cols_ref, tiles_ref, blocks_ref, out_ref, base):
    per_row = tiles_ref.shape[1]
    half = blocks_ref.shape[0] // 3
    count = out_ref.shape[0] // LANES
    group = lax.axis_index("grp").astype(jnp.int32)

    for i in range(count):
        r = base + i
        left = jnp.concatenate([tiles_ref[r, t] for t in range(per_row)], axis=1)
        right = jnp.concatenate([blocks_ref[cols_ref[t, r]] for t in range(per_row)], axis=0)
        product = jnp.dot(left, right, preferred_element_type=jnp.float32)
        own = blocks_ref[half + r % half].astype(jnp.float32)
        own = jnp.where(group == r // half, own, 0.0)
        out_ref[i * LANES : (i + 1) * LANES, :] = own - 0.5 * product


def first_body(cols_ref, tiles_ref, outer_ref, own_ref, inner_ref, out_ref, blocks_ref):
    half = own_ref.shape[0]
    place = lax.axis_index("dev")
    odd = lax.rem(place, 2) == 1
    ends = (place == 0) | (place == lax.axis_size("dev") - 1)
    outer = jnp.where(ends, jnp.zeros(own_ref.shape, own_ref.dtype), outer_ref[...])
    blocks_ref[half : 2 * half] = own_ref[...]
    blocks_ref[pl.ds(jnp.where(odd, 2 * half, 0), half)] = outer
    blocks_ref[pl.ds(jnp.where(odd, 0, 2 * half), half)] = inner_ref[...]
    product_rows(cols_ref, tiles_ref, blocks_ref, out_ref, 0)


def first_rows(cols, tiles, outer, own, inner, count):
    half = own.shape[0]
    return pl.pallas_call(
        first_body,
        out_shape=(
            jax.ShapeDtypeStruct((count * LANES, LANES), jnp.float32),
            jax.ShapeDtypeStruct((3 * half, LANES, LANES), own.dtype),
        ),
        in_specs=[SMEM_SPEC] + [VMEM_SPEC] * 4,
        out_specs=(VMEM_SPEC, VMEM_SPEC),
        compiler_params=PARAMS,
        name="first_rows",
    )(cols, tiles, outer, own, inner)


def more_body(cols_ref, tiles_ref, blocks_ref, out_ref, *, base):
    product_rows(cols_ref, tiles_ref, blocks_ref, out_ref, base)


def more_rows(cols, tiles, blocks, base, count):
    return pl.pallas_call(
        functools.partial(more_body, base=base),
        out_shape=jax.ShapeDtypeStruct((count * LANES, LANES), jnp.float32),
        in_specs=[SMEM_SPEC] + [VMEM_SPEC] * 2,
        out_specs=VMEM_SPEC,
        compiler_params=PARAMS,
        name="more_rows",
    )(cols, tiles, blocks)


def combine_body(*refs, first):
    out_ref, buffer, sems = refs[-3:]
    mine_ref, theirs_ref = refs[:2]
    each = buffer.shape[0] // PIECES
    copies = []
    for p in range(PIECES):
        rows = slice(p * each, (p + 1) * each)
        buffer[rows, :] = (mine_ref[rows, :] + theirs_ref[rows, :]).astype(buffer.dtype)
        target = out_ref.at[pl.ds(first + p * each, each)]
        copies.append(pltpu.make_async_copy(buffer.at[pl.ds(p * each, each)], target, sems.at[p]))
        copies[-1].start()
    for copy in copies:
        copy.wait()


def combine(pairs, out, rows, first, dtype):
    parts = [part for pair in pairs for part in pair]
    count, width = sum(mine.shape[0] for mine, _ in pairs), parts[0].shape[1]
    anywhere = pl.BlockSpec(memory_space=pltpu.HBM)
    before = [] if out is None else [out]
    return pl.pallas_call(
        functools.partial(combine_body, first=first),
        out_shape=jax.ShapeDtypeStruct((rows, width), dtype),
        in_specs=[VMEM_SPEC] * len(parts) + [anywhere] * len(before),
        out_specs=anywhere,
        input_output_aliases={len(parts): 0} if before else {},
        scratch_shapes=[pltpu.VMEM((count, width), dtype), pltpu.SemaphoreType.DMA((PIECES,))],
        compiler_params=PARAMS,
        name="combine",
    )(*parts, *before)


def per_device(coarse_emb, req_ids, fine_slot, tiles, tile_cols):
    groups, devices = lax.axis_size("grp"), lax.axis_size("dev")
    slots = req_ids.shape[3]
    width = coarse_emb.shape[1]
    row_blocks = tiles.shape[0]
    lists, table, index = start(req_ids[0, 0].T, coarse_emb, fine_slot.reshape(-1, LANES))
    tiles, cols = load(tiles[:, 0], tile_cols[:, 0].T)
    asked = lax.all_to_all(
        lists.reshape(devices, 1, slots), "dev", split_axis=0, concat_axis=0, tiled=True
    )
    wanted = gather(asked, table)
    received = lax.all_to_all(
        wanted.reshape(devices, slots, width), "dev", split_axis=0, concat_axis=0, tiled=True
    )
    lifted = lift(index, received.reshape(devices * slots, width))
    inner = [(i, i ^ 1) for i in range(devices)]
    outer = []
    for g in range(groups):
        outer += [(g * devices + i, g * devices + ((i + 1) ^ 1) - 1) for i in range(1, devices - 1)]
        outer += [(g * devices + i, (g ^ 1) * devices + i) for i in (0, devices - 1)]
    from_outer = lax.ppermute(lifted, ("grp", "dev"), outer).reshape(-1, LANES, width)
    from_inner = lax.ppermute(lifted, "dev", inner).reshape(-1, LANES, width)
    own = lifted.reshape(-1, LANES, width)
    parts = []
    base = 0
    for c, count in enumerate(CHUNKS):
        if c == 0:
            mine, blocks = first_rows(cols, tiles, from_outer, own, from_inner, count)
        else:
            mine = more_rows(cols, tiles, blocks, base, count)
        parts.append((mine, lax.ppermute(mine, "grp", [(0, 1), (1, 0)])))
        base += count
    rows = row_blocks * LANES
    out, base = None, 0
    for part in parts:
        out = combine([part], out, rows, base, lifted.dtype)
        base += part[0].shape[0]
    return out


def solution(mesh):
    return jax.shard_map(
        per_device,
        mesh=mesh,
        in_specs=(
            P("dev", None),
            P("dev", "grp", None, None),
            P("dev", "grp", None),
            P("dev", "grp", None, None, None),
            P("dev", "grp", None),
        ),
        out_specs=P("dev", None),
        check_vma=False,
    )
```
